128 devices in a mesh: ctx: 8 (over y, z_hi), tensor: 16 (over z_lo, x, core).
Axes of the slice: x: 4, y: 4, z: 4 (z_hi: 2, z_lo: 2; z = z_hi * 2 + z_lo), core: 2. Of those that a mesh axis runs over, the one named last changes fastest.
Arguments:
- tokens: bfloat16 [16384, 4096], P('ctx'), may hold values from -6 to 6
- norm_gain: float32 [4096], replicated, may hold values from 0.1 to 1.9
- w_in: bfloat16 [4096, 3, 4096], P(None, None, 'tensor'), may hold values from -0.09375 to 0.09375
- short_taps: float32 [3, 3, 4096], P(None, None, 'tensor'), may hold values from -3 to 3
- filter_taps: float32 [128, 4096], P(None, 'tensor'), may hold values from -0.2 to 0.2
- filter_decay: float32 [4096], P('tensor'), may hold values from 0.00234375 to 0.03125
- skip_gain: float32 [4096], P('tensor'), may hold values from -2 to 2
- w_out: bfloat16 [4096, 4096], P('tensor'), may hold values from -0.09375 to 0.09375
- slot_span: int32 [16], replicated, may hold values from 0 to 15, as said below
- span_reset: int32 [16], replicated, may hold values from 0 to 1, as said below
Outputs:
- block_out: bfloat16 [16384, 4096], P(('ctx', 'tensor'))
The draws below stay inside these ranges and needn't reach their ends.
Inputs may be any that keep to these rules, and one draw needn't show every extreme that they name: slot_span is a permutation of 0 to 15; for each ctx index d its entries 2d and 2d + 1 name the spans in that index's rows, with slot_span[2d] < 8 and slot_span[2d + 1] = 15 - slot_span[2d]. `span_reset`: some span after the first has a reset and some has none.
All inputs are finite; a program needn't handle non-finite values.
Results may differ from the reference program's by a relative error of at most 0.022.
Values may be sent and summed in bfloat16 or wider, within the bound.
A program may use at most 192 MiB of HBM per device.

```python
import math
import jax
import jax.numpy as jnp
from jax import lax

D = 4096
TAPS = 128
SPAN = 1024
NCHUNK = 16
TOKENS = 16384
DT = 256


def draw_slot_span(key, part):
    half_count = NCHUNK // 2
    order = jax.random.permutation(key, half_count).astype(jnp.int32)
    later = (NCHUNK - 1 - order).astype(jnp.int32)
    return jnp.stack([order, later], axis=1).reshape(NCHUNK).astype(jnp.int32)


def draw_span_reset(key, part):
    key_one, key_two = jax.random.split(key)
    coins = jax.random.randint(key_one, (NCHUNK,), 0, 4)
    chosen = jax.random.randint(key_two, (), 1, NCHUNK)
    other = chosen % (NCHUNK - 1) + 1
    index = jnp.arange(NCHUNK, dtype=jnp.int32)
    drawn = (coins == 0).astype(jnp.int32)
    return jnp.where(index == chosen, 1, jnp.where(index == other, 0, drawn)).astype(jnp.int32)


def draw_filter_taps(key, part):
    own_key = jax.random.fold_in(key, 7)
    key_sign, key_flip, key_size = jax.random.split(own_key, 3)
    channel_sign = jnp.where(jax.random.bernoulli(key_sign, 0.5, (1, D)), 1.0, -1.0).astype(jnp.float32)
    lag_share = jnp.arange(TAPS, dtype=jnp.float32)[:, None] / (TAPS - 1)
    flipped = jax.random.bernoulli(key_flip, 0.25, (TAPS, D))
    magnitude = jax.random.uniform(key_size, (TAPS, D), jnp.float32, 0.3, 1.0)
    ramp = 0.1 + 0.9 * lag_share
    signs = jnp.where(flipped, -channel_sign, channel_sign)
    return (0.2 * ramp * magnitude * signs).astype(jnp.float32)


def block_scale(stream_key, extent, pieces, low, high):
    loudness = 1.0
    for position, parts in pieces:
        heights = jax.random.uniform(jax.random.fold_in(jax.random.fold_in(stream_key, 6), position), (parts,), jnp.float32, low / len(pieces), high / len(pieces))
        loudness = loudness * jnp.repeat(jnp.exp(heights), extent[position] // parts).reshape((-1,) + (1,) * (len(extent) - 1 - position))
    return loudness


def normal_values(stream_key, shape, scale, reach, pieces=(), held_as=jnp.bfloat16):
    result = scale * jax.random.normal(stream_key, shape, jnp.float32)
    if pieces:
        result = result * block_scale(stream_key, shape, pieces, -0.22, 0.18)
    return jnp.clip(result, -reach, reach).astype(held_as)


def setup_inputs(seed: int = 0) -> dict:
    key_of = jax.random.split(jax.random.key(seed), 11)
    tokens = normal_values(key_of[0], (TOKENS, D), 1.0, 6.0, ((0, 8),))
    norm_gain = jnp.clip(1.0 + 0.18 * jax.random.normal(key_of[1], (D,), jnp.float32), 0.1, 1.9)
    w_in = normal_values(key_of[2], (D, 3, D), D ** -0.5, 0.09375, ((2, 16),))
    short_taps = normal_values(key_of[3], (3, 3, D), 0.6, 3.0, ((2, 16),), jnp.float32)
    filter_taps = draw_filter_taps(jax.random.fold_in(key_of[10], 71), 0)
    filter_decay = jnp.clip(jnp.exp(math.log(0.03125) - 2.5902671 * jax.random.uniform(key_of[5], (D,), jnp.float32) ** block_scale(key_of[5], (D,), ((0, 16),), -0.2, 0.2)), 0.00234375, 0.03125)
    skip_gain = normal_values(key_of[6], (D,), 0.5, 2.0, ((0, 16),), jnp.float32)
    w_out = normal_values(key_of[7], (D, D), D ** -0.5, 0.09375, ((0, 16),))
    slot_span = draw_slot_span(jax.random.fold_in(key_of[10], 71), 0)
    span_reset = draw_span_reset(jax.random.fold_in(key_of[10], 71), 0)
    return dict(tokens=tokens, norm_gain=norm_gain, w_in=w_in, short_taps=short_taps, filter_taps=filter_taps, filter_decay=filter_decay, skip_gain=skip_gain, w_out=w_out, slot_span=slot_span, span_reset=span_reset)


epsilon = 1e-06

def reference(tokens, norm_gain, w_in, short_taps, filter_taps, filter_decay, skip_gain, w_out, slot_span, span_reset):
    floats = tokens.astype(jnp.float32)
    normed = (floats * lax.rsqrt(lax.optimization_barrier(jnp.mean(floats * floats, axis=1, keepdims=True)) + epsilon) * norm_gain[None, :]).astype(jnp.bfloat16)
    projected = jnp.dot(normed, w_in.reshape(D, 3 * D), preferred_element_type=jnp.float32).astype(jnp.bfloat16)
    projected = projected.reshape(NCHUNK, SPAN, 3, D)
    slot_ids = jnp.arange(NCHUNK, dtype=jnp.int32)
    slot_of = jnp.zeros((NCHUNK,), jnp.int32).at[slot_span].set(slot_ids)
    lag_index = jnp.arange(TAPS, dtype=jnp.float32)
    response = filter_taps * jnp.exp(-filter_decay[None, :] * lag_index[:, None])
    conv_len = TAPS - 1 + SPAN

    def one_slot(slot):
        span_id = slot_span[slot]
        source = slot_of[jnp.maximum(span_id - 1, 0)]
        use_tail = jnp.logical_and(span_id > 0, span_reset[span_id] == 0)
        tail_rows = lax.dynamic_index_in_dim(projected, source, 0, keepdims=False)[SPAN - TAPS - 1:]
        tail_rows = jnp.where(use_tail, tail_rows.astype(jnp.float32), jnp.zeros_like(tail_rows, dtype=jnp.float32))
        own_rows = lax.dynamic_index_in_dim(projected, slot, 0, keepdims=False).astype(jnp.float32)
        extended = jnp.concatenate([tail_rows, own_rows], axis=0)
        smoothed = short_taps[0][None] * extended[2:2 + conv_len] + short_taps[1][None] * extended[1:1 + conv_len] + short_taps[2][None] * extended[0:conv_len]
        gate_query = smoothed[TAPS - 1:, 0]
        mixed_in = smoothed[:, 1] * smoothed[:, 2]

        def add_lag(offset, running):
            shifted = lax.dynamic_slice_in_dim(mixed_in, jnp.int32(TAPS - 1) - offset.astype(jnp.int32), SPAN, 0)
            return running + lax.dynamic_index_in_dim(response, offset, 0, keepdims=False)[None, :] * shifted
        filtered = lax.fori_loop(0, TAPS, add_lag, jnp.zeros((SPAN, D), jnp.float32))
        gated = gate_query * (filtered + skip_gain[None, :] * mixed_in[TAPS - 1:])
        return gated.astype(jnp.bfloat16)
    gated = lax.map(one_slot, slot_ids).reshape(TOKENS, D)

    def add_group(group_idx, running):
        first_col = group_idx * DT
        gate_cols = lax.dynamic_slice_in_dim(gated, first_col, DT, 1)
        weight_rows = lax.dynamic_slice_in_dim(w_out, first_col, DT, 0)
        partial_value = jnp.dot(gate_cols, weight_rows, preferred_element_type=jnp.float32).astype(jnp.bfloat16)
        partial_value = lax.optimization_barrier(partial_value)
        return running + partial_value.astype(jnp.float32)
    mixed = lax.fori_loop(0, D // DT, add_group, jnp.zeros((TOKENS, D), jnp.float32))
    return (floats + mixed).astype(jnp.bfloat16)
```

```python
import functools

import jax
import jax.numpy as jnp
import numpy as np
from jax import lax
from jax.experimental import pallas as pl
from jax.experimental.pallas import tpu as pltpu
from jax.sharding import PartitionSpec as P

epsilon = 1e-06
F32 = jnp.float32
BF16 = jnp.bfloat16
MESH = pl.DeviceIdType.MESH
HALO = 160


def split(value):
    high = value.astype(BF16)
    low = (value - high.astype(F32)).astype(BF16)
    return high, low


def transforms():
    points = 256
    k = np.arange(128)[:, None]
    n = np.arange(points)[None, :]
    forward = np.zeros((points, points))
    forward[:128] = np.cos(2 * np.pi * k * n / points)
    forward[128:] = np.sin(2 * np.pi * k * n / points)
    forward[128] = np.cos(np.pi * n[0])
    weight = np.full((points, 1), 2.0 / points)
    weight[0] = weight[128] = 1.0 / points
    inverse = (forward * weight)[:, 128:].T

    def halves(matrix):
        high = matrix.astype(jnp.bfloat16)
        low = (matrix - high.astype(np.float64)).astype(jnp.bfloat16)
        return np.stack([high, low])

    return halves(forward), halves(inverse)


def dot(a, b):
    return jnp.dot(a, b, preferred_element_type=F32)


def kernel(
    tokens,
    gain,
    w_in,
    short,
    taps,
    decay,
    skip,
    w_out,
    fwd,
    inv,
    slot_span,
    span_reset,
    out,
    tok,
    scaled,
    win,
    pr,
    spec,
    halo,
    gsend,
    grecv,
    wg,
    part,
    recv,
    own,
    tok_sem,
    win_sem,
    loc_sem,
    h_send,
    h_recv,
    g_send,
    g_recv,
    w_send,
    w_recv,
    r_send,
    r_recv,
):
    ctx = lax.axis_index("ctx")
    ten = lax.axis_index("tensor")
    z = ten // 8
    x = (ten // 2) % 4
    core = ten % 2
    oz = 1 - z
    oc = 1 - core
    octx = ctx + 1 - 2 * (ctx % 2)
    right = (x + 1) % 4
    left = (x + 3) % 4
    far = (x + 2) % 4

    def place(z_, x_, c_):
        return z_ * 8 + x_ * 2 + c_

    partner = (ctx, place(z, x, oc))
    zsame = (ctx, place(oz, x, core))
    zcross = (ctx, place(oz, x, oc))
    zother = (octx, place(oz, x, core))
    to_right = (ctx, place(z, right, core))
    to_left = (ctx, place(z, left, core))
    circle = [((ctx + d) % 8, ten) for d in range(1, 8)]
    peers = [partner, zsame, zcross, zother, to_right, to_left] + circle

    def block_of(i):
        j = i - 2
        s = jnp.where(i < 2, jnp.where(i == 0, oz, z), jnp.where(j < 3, oz, z))
        q = jnp.where(i < 2, 3, 2 - j % 3)
        return s, q

    def fetch(i):
        s, q = block_of(i)
        row = pl.multiple_of(s * 1024 + q * 256, 256)
        return pltpu.make_async_copy(
            tokens.at[pl.ds(row, 256)], tok.at[i % 2], tok_sem.at[i % 2]
        )

    barrier = pltpu.get_barrier_semaphore()
    for peer in peers:
        pl.semaphore_signal(barrier, inc=1, device_id=peer, device_id_type=MESH)
    fetch(jnp.int32(0)).start()
    win_copy = pltpu.make_async_copy(w_in, win, win_sem.at[0])
    win_copy.start()
    own_group = z * 2 + core
    own_rows = pl.multiple_of(own_group * 256, 256)
    wg_copy = pltpu.make_async_copy(w_out, wg.at[pl.ds(own_rows, 256)], loc_sem.at[0])
    wg_copy.start()
    tok_row = pl.multiple_of(ten * 128, 128)
    own_copy = pltpu.make_async_copy(tokens.at[pl.ds(tok_row, 128)], own, loc_sem.at[1])
    own_copy.start()
    pl.semaphore_wait(barrier, len(peers))

    pieces = [0, 2, 1, 3]

    def w_copy(index, source, rows, piece, peer):
        cols = pl.ds(piece * 1024, 1024)
        if source is None:
            src = wg.at[pl.ds(rows, 256), cols]
        else:
            src = source.at[:, cols]
        return pltpu.make_async_remote_copy(
            src_ref=src,
            dst_ref=wg.at[pl.ds(rows, 256), cols],
            send_sem=w_send.at[index],
            recv_sem=w_recv.at[index],
            device_id=peer,
            device_id_type=MESH,
        )

    z_rows = pl.multiple_of((oz * 2 + core) * 256, 256)
    w_partner = [w_copy(i, w_out, own_rows, p, partner) for i, p in enumerate(pieces)]
    w_z = [
        w_copy(4 + i, w_out, own_rows, p, zsame if p < 2 else zother)
        for i, p in enumerate(pieces)
    ]
    w_relay = [w_copy(8 + i, None, z_rows, p, partner) for i, p in enumerate(pieces)]
    for copy in w_z:
        copy.start()
    for copy in w_partner:
        copy.start()

    lag = lax.broadcasted_iota(jnp.int32, (128, 256), 0)
    response = taps[...] * jnp.exp(-decay[...] * lag.astype(F32))
    response = response + jnp.where(lag == 0, skip[...], 0.0)
    r_high, r_low = split(response)
    spectrum = (
        dot(fwd[0, :, :128], r_high) + dot(fwd[1, :, :128], r_high) + dot(fwd[0, :, :128], r_low)
    )
    cos_part = spectrum[:128]
    sin_part = spectrum[128:]
    spec[0] = cos_part
    spec[1] = jnp.where(lag == 0, 0.0, sin_part)
    spec[2] = jnp.where(lag == 0, sin_part, cos_part)

    def project(i):
        s, q = block_of(i)
        slot = i % 2
        fetch(i).wait()
        square = jnp.zeros((256, 128), F32)
        for chunk in range(8):
            cols = pl.ds(chunk * 512, 512)
            value = tok[slot, :, cols].astype(F32)
            scaled[:, cols] = (value * gain[:, cols]).astype(BF16)
            value = value * value
            for lane in range(4):
                square = square + value[:, lane * 128 : lane * 128 + 128]
        scale = lax.rsqrt(jnp.sum(square, axis=1, keepdims=True) * (1.0 / 4096) + epsilon)
        row = pl.multiple_of(8 + q * 256, 8)
        for p in range(3):
            pr[p, s, pl.ds(row, 256), :] = dot(scaled[...], win[p]) * scale

    def smooth(p, value, rows):
        return (
            short[0, pl.ds(p, 1), :] * value[8 : 8 + rows]
            + short[1, pl.ds(p, 1), :] * value[7 : 7 + rows]
            + short[2, pl.ds(p, 1), :] * value[6 : 6 + rows]
        )

    def tail_copies(s):
        index = ctx * 2 + s
        return [
            pltpu.make_async_remote_copy(
                src_ref=halo.at[index],
                dst_ref=halo.at[index],
                send_sem=h_send.at[d * 2 + s],
                recv_sem=h_recv.at[d * 2 + s],
                device_id=circle[d],
                device_id_type=MESH,
            )
            for d in range(7)
        ]

    def tail_step(i, carry):
        fetch(i + 1).start()
        project(i)
        s, _ = block_of(i)
        key = smooth(1, pr[1, s, pl.ds(896, 136), :], 128)
        val = smooth(2, pr[2, s, pl.ds(896, 136), :], 128)
        index = ctx * 2 + s
        halo[index, pl.ds(0, 128), :] = (key * val).astype(BF16)
        last = [pr[p, s, pl.ds(1024, 8), :] for p in range(3)]
        last.append(jnp.zeros((8, 256), F32))
        halo[index, pl.ds(128, 32), :] = jnp.concatenate(last, axis=0).astype(BF16)
        for copy in tail_copies(s):
            copy.start()
        return carry

    def convolve(mixed, query):
        high, low = split(mixed)
        outs = []
        for w in range(2):
            h = high[w * 128 : w * 128 + 256]
            l = low[w * 128 : w * 128 + 256]
            freq = dot(fwd[0], h) + dot(fwd[1], h) + dot(fwd[0], l)
            a = freq[:128]
            b = freq[128:]
            y = jnp.concatenate([a * spec[0] - b * spec[1], a * spec[1] + b * spec[2]], axis=0)
            y_high, y_low = split(y)
            outs.append(dot(inv[0], y_high) + dot(inv[1], y_high) + dot(inv[0], y_low))
        return (query * jnp.concatenate(outs, axis=0)).astype(BF16)

    own_cols = pl.ds(pl.multiple_of(own_group * 256, 256), 256)

    def gated_copy(index, send_row, peer, q):
        return pltpu.make_async_remote_copy(
            src_ref=gsend.at[pl.ds(send_row, 128)],
            dst_ref=grecv.at[pl.ds(pl.multiple_of(q * 128, 128), 128), own_cols],
            send_sem=g_send.at[index * 4 + q],
            recv_sem=g_recv.at[index * 4 + q],
            device_id=peer,
            device_id_type=MESH,
        )

    def gated_other(q):
        base = pl.multiple_of(q * 256, 256)
        same_row = pl.multiple_of(base + core * 128, 128)
        cross_row = pl.multiple_of(base + oc * 128, 128)
        return [gated_copy(0, same_row, zsame, q), gated_copy(1, cross_row, zcross, q)]

    def gated_mine(q):
        row = pl.multiple_of(1024 + q * 256 + oc * 128, 128)
        return [gated_copy(2, row, partner, q)]

    def emit(role, q, gated):
        row = pl.multiple_of(role * 1024 + q * 256, 256)
        gsend[pl.ds(row, 256), :] = gated
        if role == 0:
            copies = gated_other(q)
        else:
            keep = pl.multiple_of(row + core * 128, 128)
            grecv[pl.ds(pl.multiple_of(q * 128, 128), 128), own_cols] = gsend[pl.ds(keep, 128), :]
            copies = gated_mine(q)
        for copy in copies:
            copy.start()

    def main_step(role, last):
        def body(j, carry):
            i = 2 + role * 3 + j
            if last:

                @pl.when(j < 2)
                def _():
                    fetch(i + 1).start()
            else:
                fetch(i + 1).start()
            project(i)
            s = z if role else oz
            q = 3 - j
            wide = pl.ds(pl.multiple_of(q * 256 - 128, 128), 392)
            narrow = pl.ds(pl.multiple_of(q * 256, 256), 264)
            key = smooth(1, pr[1, s, wide, :], 384)
            val = smooth(2, pr[2, s, wide, :], 384)
            query = smooth(0, pr[0, s, narrow, :], 256)
            emit(role, q, convolve(key * val, query))
            return carry

        return body

    win_copy.wait()
    lax.fori_loop(0, 2, tail_step, 0)
    lax.fori_loop(0, 3, main_step(0, False), 0)
    lax.fori_loop(0, 3, main_step(1, True), 0)

    for s in range(2):
        for copy in tail_copies(s):
            copy.wait()
    for role in range(2):
        s = z if role else oz
        span = slot_span[2 * ctx + s]
        source = jnp.int32(0)
        for j in range(16):
            source = source + jnp.where(slot_span[j] == span - 1, j, 0)
        used = jnp.logical_and(span > 0, span_reset[span] == 0)
        mask = jnp.where(used, 1.0, 0.0)
        before = halo[source].astype(F32) * mask
        for p in range(3):
            pr[p, s, pl.ds(0, 8), :] = before[128 + p * 8 : 136 + p * 8]
        window = pl.ds(0, 264)
        key = smooth(1, pr[1, s, window, :], 256)
        val = smooth(2, pr[2, s, window, :], 256)
        query = smooth(0, pr[0, s, window, :], 256)
        mixed = jnp.concatenate([before[:128], key * val], axis=0)
        emit(role, jnp.int32(0), convolve(mixed, query))

    for i in range(4):
        w_z[i].wait()
        w_relay[i].start()
    wg_copy.wait()
    for q in range(4):
        for copy in gated_other(q) + gated_mine(q):
            copy.wait()

    def r_copy(index, block, piece, peer):
        cols = pl.ds(piece * 1024, 1024)
        return pltpu.make_async_remote_copy(
            src_ref=part.at[block, :, cols],
            dst_ref=recv.at[index],
            send_sem=r_send.at[index],
            recv_sem=r_recv.at[index],
            device_id=peer,
            device_id_type=MESH,
        )

    sums = []
    for half in range(2):
        a, b = half, 2 + half
        sums.append(
            [
                r_copy(6 * half + 0, far, a, to_right),
                r_copy(6 * half + 1, far, b, to_left),
                r_copy(6 * half + 2, right, b, to_right),
                r_copy(6 * half + 3, left, a, to_left),
                r_copy(6 * half + 4, right, a, to_right),
                r_copy(6 * half + 5, left, b, to_left),
            ]
        )
    for half in range(2):
        for i in (2 * half, 2 * half + 1):
            w_partner[i].wait()
            w_relay[i].wait()
            piece = pieces[i]

            def columns(j, carry, piece=piece):
                cols = pl.ds(pl.multiple_of(piece * 1024 + j * 256, 256), 256)
                value = dot(grecv[...], wg[:, cols]).astype(BF16)
                for q in range(4):
                    part[q, :, cols] = value[q * 128 : q * 128 + 128]
                return carry

            lax.fori_loop(0, 4, columns, 0)
        for copy in sums[half][:4]:
            copy.start()
    for half in range(2):
        for index, block, piece in ((0, right, half), (1, left, 2 + half)):
            sums[half][index].wait()
            cols = pl.ds(piece * 1024, 1024)
            part[block, :, cols] = (
                part[block, :, cols].astype(F32) + recv[6 * half + index].astype(F32)
            ).astype(BF16)
            sums[half][4 + index].start()
    own_copy.wait()
    for half in range(2):
        for piece, first, second in ((half, 3, 4), (2 + half, 2, 5)):
            sums[half][first].wait()
            sums[half][second].wait()
            cols = pl.ds(piece * 1024, 1024)
            total = part[x, :, cols].astype(F32) + recv[6 * half + first].astype(F32)
            total = total + recv[6 * half + second].astype(F32)
            out[:, cols] = (own[:, cols].astype(F32) + total).astype(BF16)


def shards(
    tokens,
    norm_gain,
    w_in,
    short_taps,
    filter_taps,
    filter_decay,
    skip_gain,
    w_out,
    slot_span,
    span_reset,
):
    fwd, inv = transforms()
    hbm = pl.BlockSpec(memory_space=pl.ANY)
    vmem = pl.BlockSpec(memory_space=pltpu.VMEM)
    smem = pl.BlockSpec(memory_space=pltpu.SMEM)
    return pl.pallas_call(
        kernel,
        out_shape=jax.ShapeDtypeStruct((128, 4096), BF16),
        in_specs=[hbm, vmem, hbm, vmem, vmem, vmem, vmem, hbm, vmem, vmem, smem, smem],
        out_specs=vmem,
        scratch_shapes=[
            pltpu.VMEM((2, 256, 4096), BF16),
            pltpu.VMEM((256, 4096), BF16),
            pltpu.VMEM((3, 4096, 256), BF16),
            pltpu.VMEM((3, 2, 1032, 256), F32),
            pltpu.VMEM((3, 128, 256), F32),
            pltpu.VMEM((16, HALO, 256), BF16),
            pltpu.VMEM((2048, 256), BF16),
            pltpu.VMEM((512, 1024), BF16),
            pltpu.VMEM((1024, 4096), BF16),
            pltpu.VMEM((4, 128, 4096), BF16),
            pltpu.VMEM((12, 128, 1024), BF16),
            pltpu.VMEM((128, 4096), BF16),
            pltpu.SemaphoreType.DMA((2,)),
            pltpu.SemaphoreType.DMA((1,)),
            pltpu.SemaphoreType.DMA((2,)),
            pltpu.SemaphoreType.DMA((14,)),
            pltpu.SemaphoreType.DMA((14,)),
            pltpu.SemaphoreType.DMA((12,)),
            pltpu.SemaphoreType.DMA((12,)),
            pltpu.SemaphoreType.DMA((12,)),
            pltpu.SemaphoreType.DMA((12,)),
            pltpu.SemaphoreType.DMA((12,)),
            pltpu.SemaphoreType.DMA((12,)),
        ],
        compiler_params=pltpu.CompilerParams(
            collective_id=0, has_side_effects=True, vmem_limit_bytes=60 * 1024 * 1024
        ),
    )(
        tokens,
        norm_gain.reshape(1, -1),
        jnp.transpose(w_in, (1, 0, 2)),
        short_taps,
        filter_taps,
        filter_decay.reshape(1, -1),
        skip_gain.reshape(1, -1),
        w_out,
        jnp.asarray(fwd),
        jnp.asarray(inv),
        slot_span,
        span_reset,
    )


def solution(mesh):
    in_specs = (
        P("ctx", None),
        P(),
        P(None, None, "tensor"),
        P(None, None, "tensor"),
        P(None, "tensor"),
        P("tensor"),
        P("tensor"),
        P("tensor", None),
        P(),
        P(),
    )
    out_specs = P(("ctx", "tensor"), None)
    return jax.shard_map(shards, mesh=mesh, in_specs=in_specs, out_specs=out_specs, check_vma=False)
```

```python
import jax
import jax.numpy as jnp
import numpy as np
from jax import lax
from jax.experimental import pallas as pl
from jax.experimental.pallas import tpu as pltpu
from jax.sharding import PartitionSpec as P

epsilon = 1e-06
F32 = jnp.float32
BF16 = jnp.bfloat16
MESH = pl.DeviceIdType.MESH
HALO = 144


def split(value):
    high = value.astype(BF16)
    low = (value - high.astype(F32)).astype(BF16)
    return high, low


def transforms():
    points = 256
    k = np.arange(128)[:, None]
    n = np.arange(points)[None, :]
    forward = np.zeros((points, points))
    forward[:128] = np.cos(2 * np.pi * k * n / points)
    forward[128:] = np.sin(2 * np.pi * k * n / points)
    forward[128] = np.cos(np.pi * n[0])
    weight = np.full((points, 1), 2.0 / points)
    weight[0] = weight[128] = 1.0 / points
    inverse = (forward * weight)[:, 128:].T

    def halves(matrix):
        high = matrix.astype(jnp.bfloat16)
        low = (matrix - high.astype(np.float64)).astype(jnp.bfloat16)
        return np.stack([high, low])

    return halves(forward), halves(inverse)


def dot(a, b):
    return jnp.dot(a, b, preferred_element_type=F32)


def kernel(
    tokens,
    gain,
    w_in,
    short,
    taps,
    decay,
    skip,
    w_out,
    fwd,
    inv,
    slot_span,
    span_reset,
    out,
    tok,
    scaled,
    win,
    pr,
    spec,
    column,
    across,
    gsend,
    grecv,
    wg,
    part,
    recv,
    own,
    mix,
    gate,
    prods,
    tok_sem,
    win_sem,
    loc_sem,
    y_send,
    y_recv,
    z_send,
    z_recv,
    g_send,
    g_recv,
    w_send,
    w_recv,
    r_send,
    r_recv,
):
    ctx = lax.axis_index("ctx")
    ten = lax.axis_index("tensor")
    y = ctx // 2
    zh = ctx % 2
    z = ten // 8
    x = (ten // 2) % 4
    core = ten % 2
    oz = 1 - z
    oc = 1 - core
    octx = y * 2 + 1 - zh
    right = (x + 1) % 4
    left = (x + 3) % 4
    far = (x + 2) % 4

    def place(z_, x_, c_):
        return z_ * 8 + x_ * 2 + c_

    partner = (ctx, place(z, x, oc))
    zsame = (ctx, place(oz, x, core))
    zcross = (ctx, place(oz, x, oc))
    zother = (octx, place(oz, x, core))
    zfar = (octx, ten)
    to_right = (ctx, place(z, right, core))
    to_left = (ctx, place(z, left, core))
    y_peers = [(((y + d) % 4) * 2 + zh, ten) for d in (2, 1, 3)]
    peers = [partner, zsame, zcross, zother, zfar, to_right, to_left] + y_peers

    first = [(oz, 880, 144), (z, 880, 144)]
    second = [(oz, 768, 112), (z, 768, 112)]

    def block_of(i):
        j = i - 2
        return jnp.where(j < 3, oz, z), 2 - j % 3

    def pieces_of(i):
        if isinstance(i, int) and i < 2:
            return (first, second)[i]
        s, q = block_of(i)
        return [(s, q * 256, 256)]

    def fetch(i):
        offset = 0
        copies = []
        for s, start, count in pieces_of(i):
            row = pl.multiple_of(s * 1024 + start, 16)
            index = (i % 2) * 2 + len(copies)
            copies.append(
                pltpu.make_async_copy(
                    tokens.at[pl.ds(row, count)],
                    tok.at[i % 2, pl.ds(offset, count)],
                    tok_sem.at[index],
                )
            )
            offset += count
        return copies

    def start(copies):
        for copy in copies:
            copy.start()

    def wait(copies):
        for copy in copies:
            copy.wait()

    barrier = pltpu.get_barrier_semaphore()
    for peer in peers:
        pl.semaphore_signal(barrier, inc=1, device_id=peer, device_id_type=MESH)
    own_group = z * 2 + core
    own_rows = pl.multiple_of(own_group * 256, 256)
    wg_copy = pltpu.make_async_copy(w_out, wg.at[pl.ds(own_rows, 256)], loc_sem.at[0])
    wg_copy.start()
    start(fetch(0))
    win_copies = [pltpu.make_async_copy(w_in.at[p], win.at[p], win_sem.at[p]) for p in range(3)]
    start(win_copies)
    start(fetch(1))
    tok_row = pl.multiple_of(ten * 128, 128)
    own_copy = pltpu.make_async_copy(tokens.at[pl.ds(tok_row, 128)], own, loc_sem.at[1])
    own_copy.start()
    wg_copy.wait()
    pl.semaphore_wait(barrier, len(peers))

    def w_copy(index, rows, chunk, peer):
        cols = pl.ds(chunk * 512, 512)
        return pltpu.make_async_remote_copy(
            src_ref=wg.at[pl.ds(rows, 256), cols],
            dst_ref=wg.at[pl.ds(rows, 256), cols],
            send_sem=w_send.at[index],
            recv_sem=w_recv.at[index],
            device_id=peer,
            device_id_type=MESH,
        )

    z_rows = pl.multiple_of((oz * 2 + core) * 256, 256)
    direct = (0, 1, 7)
    w_partner = [w_copy(c, own_rows, c, partner) for c in range(8)]
    w_z = [w_copy(8 + c, own_rows, c, zsame if c in direct else zother) for c in range(8)]
    w_relay = [w_copy(16 + c, z_rows, c, partner) for c in range(8)]

    def relay(chunks):
        for c in chunks:
            w_z[c].wait_recv()
            w_relay[c].start()

    start([w_z[0], w_z[4], w_z[1], w_z[5], w_z[2]])
    start([w_partner[c] for c in (0, 4, 1, 5, 2, 6, 3, 7)])

    lag = lax.broadcasted_iota(jnp.int32, (128, 256), 0)
    response = taps[...] * jnp.exp(-decay[...] * lag.astype(F32))
    response = response + jnp.where(lag == 0, skip[...], 0.0)
    r_high, r_low = split(response)
    spectrum = (
        dot(fwd[0, :, :128], r_high) + dot(fwd[1, :, :128], r_high) + dot(fwd[0, :, :128], r_low)
    )
    cos_part = spectrum[:128]
    sin_part = spectrum[128:]
    spec[0] = cos_part
    spec[1] = jnp.where(lag == 0, 0.0, sin_part)
    spec[2] = jnp.where(lag == 0, sin_part, cos_part)

    def prepare(i):
        slot = i % 2
        rows = sum(count for _, _, count in pieces_of(i))
        square = jnp.zeros((rows, 128), F32)
        for chunk in range(8):
            cols = pl.ds(chunk * 512, 512)
            value = tok[slot, pl.ds(0, rows), cols].astype(F32)
            scaled[pl.ds(0, rows), cols] = (value * gain[:, cols]).astype(BF16)
            value = value * value
            for lane in range(4):
                square = square + value[:, lane * 128 : lane * 128 + 128]
        return lax.rsqrt(jnp.sum(square, axis=1, keepdims=True) * (1.0 / 4096) + epsilon)

    def project_part(i, p, scale):
        layout = pieces_of(i)
        rows = sum(count for _, _, count in layout)
        value = dot(scaled[pl.ds(0, rows), :], win[p]) * scale
        offset = 0
        for s, begin, count in layout:
            row = pl.multiple_of(8 + begin, 8)
            pr[p, s, pl.ds(row, count), :] = value[offset : offset + count]
            offset += count

    def project(i):
        scale = prepare(i)
        for p in range(3):
            project_part(i, p, scale)

    def smooth(p, value, rows):
        return (
            short[0, pl.ds(p, 1), :] * value[8 : 8 + rows]
            + short[1, pl.ds(p, 1), :] * value[7 : 7 + rows]
            + short[2, pl.ds(p, 1), :] * value[6 : 6 + rows]
        )

    def y_copies(s):
        index = y * 2 + s
        return [
            pltpu.make_async_remote_copy(
                src_ref=column.at[index],
                dst_ref=column.at[index],
                send_sem=y_send.at[d * 2 + s],
                recv_sem=y_recv.at[d * 2 + s],
                device_id=y_peers[d],
                device_id_type=MESH,
            )
            for d in range(3)
        ]

    line = lax.broadcasted_iota(jnp.int32, (8, 256), 0)

    def send_tail(s):
        index = y * 2 + s
        key = smooth(1, pr[1, s, pl.ds(896, 136), :], 128)
        val = smooth(2, pr[2, s, pl.ds(896, 136), :], 128)
        column[index, pl.ds(0, 128), :] = (key * val).astype(BF16)
        last = [pr[p, s, pl.ds(1024, 8), :] for p in range(3)]
        pair = jnp.where(line >= 6, last[0], pltpu.roll(last[1], 6, 0))
        column[index, pl.ds(128, 16), :] = jnp.concatenate([pair, last[2]], axis=0).astype(BF16)
        start(y_copies(s))

    def wanted(holder, s):
        span = slot_span[2 * holder + s]
        index = jnp.int32(0)
        half = jnp.int32(0)
        for j in range(16):
            hit = slot_span[j] == span - 1
            index = index + jnp.where(hit, (j // 4) * 2 + j % 2, 0)
            half = half + jnp.where(hit, (j // 2) % 2, 0)
        used = jnp.logical_and(span > 0, span_reset[span] == 0)
        return index, half, used

    z_copy = pltpu.make_async_remote_copy(
        src_ref=across.at[0],
        dst_ref=across.at[1],
        send_sem=z_send.at[0],
        recv_sem=z_recv.at[0],
        device_id=zfar,
        device_id_type=MESH,
    )

    def send_across():
        for s in range(2):
            for copy in y_copies(s):
                copy.wait_recv()
        for s in range(2):
            index, _, _ = wanted(octx, s)
            across[0, s] = column[index]
        z_copy.start()

    def to_spectrum(window):
        freq = dot(fwd[0], window)
        a = freq[:128]
        b = freq[128:]
        prod = jnp.concatenate([a * spec[0] - b * spec[1], a * spec[1] + b * spec[2]], axis=0)
        return prod.astype(BF16)

    def convolve(mixed, query):
        mixed = mixed.astype(BF16)
        outs = [dot(inv[0], to_spectrum(mixed[w * 128 : w * 128 + 256])) for w in range(2)]
        return (query * jnp.concatenate(outs, axis=0)).astype(BF16)

    own_cols = pl.ds(pl.multiple_of(own_group * 256, 256), 256)

    def gated_copy(index, send_row, peer, q):
        return pltpu.make_async_remote_copy(
            src_ref=gsend.at[pl.ds(send_row, 128)],
            dst_ref=grecv.at[pl.ds(pl.multiple_of(q * 128, 128), 128), own_cols],
            send_sem=g_send.at[index * 4 + q],
            recv_sem=g_recv.at[index * 4 + q],
            device_id=peer,
            device_id_type=MESH,
        )

    def gated_other(q):
        base = pl.multiple_of(q * 256, 256)
        same_row = pl.multiple_of(base + core * 128, 128)
        cross_row = pl.multiple_of(base + oc * 128, 128)
        return [gated_copy(0, same_row, zsame, q), gated_copy(1, cross_row, zcross, q)]

    def gated_mine(q):
        row = pl.multiple_of(1024 + q * 256 + oc * 128, 128)
        return [gated_copy(2, row, partner, q)]

    def keep(q):
        row = pl.multiple_of(1024 + q * 256 + core * 128, 128)
        grecv[pl.ds(pl.multiple_of(q * 128, 128), 128), own_cols] = gsend[pl.ds(row, 128), :]

    def smooth_block(role, q):
        s = jnp.where(role == 0, oz, z)
        wide = pl.ds(pl.multiple_of(q * 256 - 128, 128), 392)
        narrow = pl.ds(pl.multiple_of(q * 256, 256), 264)
        key = smooth(1, pr[1, s, wide, :], 384)
        val = smooth(2, pr[2, s, wide, :], 384)
        return key * val, smooth(0, pr[0, s, narrow, :], 256)

    def filter_block(role, q):
        row = pl.multiple_of(role * 1024 + q * 256, 256)
        gsend[pl.ds(row, 256), :] = convolve(*smooth_block(role, q))

    def filter_and_project(role, q, i):
        row = role * 1024 + q * 256
        mixed, query = smooth_block(role, q)
        mix[...] = mixed.astype(BF16)
        gate[...] = query
        scale = prepare(i)
        project_part(i, 0, scale)
        for w in range(2):
            prods[w] = to_spectrum(mix[pl.ds(w * 128, 256), :])
        project_part(i, 1, scale)
        for w in range(2):
            half = pl.ds(pl.multiple_of(row + w * 128, 128), 128)
            gsend[half, :] = (gate[pl.ds(w * 128, 128), :] * dot(inv[0], prods[w])).astype(BF16)
        project_part(i, 2, scale)

    def filter_first(role):
        s = oz if role == 0 else z
        index, half, used = wanted(ctx, s)
        mask_here = jnp.where(jnp.logical_and(used, half == zh), 1.0, 0.0)
        mask_across = jnp.where(jnp.logical_and(used, half != zh), 1.0, 0.0)
        before = column[index].astype(F32) * mask_here + across[1, s].astype(F32) * mask_across
        pair = before[128:136]
        pr[0, s, pl.ds(0, 8), :] = pair
        pr[1, s, pl.ds(0, 8), :] = pltpu.roll(pair, 2, 0)
        pr[2, s, pl.ds(0, 8), :] = before[136:144]
        window = pl.ds(0, 264)
        key = smooth(1, pr[1, s, window, :], 256)
        val = smooth(2, pr[2, s, window, :], 256)
        query = smooth(0, pr[0, s, window, :], 256)
        mixed = jnp.concatenate([before[:128], key * val], axis=0)
        gsend[pl.ds(role * 1024, 256), :] = convolve(mixed, query)

    wait(fetch(0))
    scale = prepare(0)
    start(fetch(2))
    for p in range(3):
        win_copies[p].wait()
        project_part(0, p, scale)
    for s in range(2):
        send_tail(s)
    wait(fetch(1))
    project(1)
    start(fetch(3))
    wait(fetch(2))
    project(2)

    def main_step(i, carry):
        j = i - 3
        role = jnp.where(j < 3, 0, 1)
        q = 3 - j % 3

        @pl.when(i < 7)
        def _():
            start(fetch(i + 1))

        wait(fetch(i))
        filter_and_project(role, q, i)

        @pl.when(j < 3)
        def _():
            start(gated_other(q))

        @pl.when(j >= 3)
        def _():
            keep(q)
            start(gated_mine(q))

        @pl.when(j == 0)
        def _():
            relay((0, 4))

        @pl.when(j == 1)
        def _():
            relay((1, 5))
            w_z[6].start()

        @pl.when(j == 2)
        def _():
            send_across()
            start([w_z[3], w_z[7]])

        @pl.when(j == 3)
        def _():
            relay((2,))

        return carry

    lax.fori_loop(3, 8, main_step, 0)
    filter_block(1, jnp.int32(1))
    keep(1)
    start(gated_mine(1))

    def r_copy(index, block, chunk, peer):
        cols = pl.ds(chunk * 512, 512)
        return pltpu.make_async_remote_copy(
            src_ref=part.at[block, :, cols],
            dst_ref=recv.at[index],
            send_sem=r_send.at[index],
            recv_sem=r_recv.at[index],
            device_id=peer,
            device_id_type=MESH,
        )

    sums = []
    for r in range(4):
        a, b = r, 4 + r
        sums.append(
            [
                (far, r_copy(6 * r + 0, far, a, to_right)),
                (far, r_copy(6 * r + 1, far, b, to_left)),
                (right, r_copy(6 * r + 2, right, b, to_right)),
                (left, r_copy(6 * r + 3, left, a, to_left)),
                (right, r_copy(6 * r + 4, right, a, to_right)),
                (left, r_copy(6 * r + 5, left, b, to_left)),
            ]
        )

    def multiply(r, begin, blocks):
        def columns(k, carry):
            cols = pl.ds(pl.multiple_of((k // 2) * 2048 + r * 512 + (k % 2) * 256, 256), 256)
            value = dot(grecv[pl.ds(begin * 128, blocks * 128), :], wg[:, cols]).astype(BF16)
            for q in range(blocks):
                part[begin + q, :, cols] = value[q * 128 : q * 128 + 128]
            return carry

        lax.fori_loop(0, 4, columns, 0)

    def send_own(r, ready):
        for block, copy in sums[r][:4]:
            if ready is None:
                copy.start()
            else:

                @pl.when(ready(block))
                def _(copy=copy):
                    copy.start()

    def add_and_send(r, index):
        block, copy = sums[r][4 + index]
        sums[r][index][1].wait_recv()
        cols = pl.ds((r + 4 * index) * 512, 512)
        part[block, :, cols] = (
            part[block, :, cols].astype(F32) + recv[6 * r + index].astype(F32)
        ).astype(BF16)
        copy.start()

    def pass_on(r, ready):
        for index in range(2):
            if ready is None:
                add_and_send(r, index)
            else:

                @pl.when(ready(sums[r][4 + index][0]))
                def _(index=index):
                    add_and_send(r, index)

    def w_ready(r):
        for c in (r, 4 + r):
            w_partner[c].wait_recv()
            w_relay[c].wait_recv()

    early = lambda block: block != 0
    late = lambda block: block == 0

    def gated_ready(q):
        for copy in gated_other(q) + gated_mine(q):
            copy.wait_recv()

    for q in (3, 2, 1):
        gated_ready(q)
    for r in range(2):
        w_ready(r)
        multiply(r, 1, 3)
        send_own(r, early)

    z_copy.wait_recv()
    filter_first(0)
    start(gated_other(0))
    filter_first(1)
    keep(0)
    start(gated_mine(0))
    relay((6,))
    gated_ready(0)
    for r in range(2):
        multiply(r, 0, 1)
        send_own(r, late)
    w_ready(2)
    multiply(2, 0, 4)
    send_own(2, None)
    relay((3, 7))
    for r in range(2):
        pass_on(r, early)
    w_ready(3)
    multiply(3, 0, 4)
    send_own(3, None)
    for r in range(2):
        pass_on(r, late)
    for r in (2, 3):
        pass_on(r, None)
    own_copy.wait()
    for r in range(4):
        for chunk, near, passed in ((r, 3, 4), (4 + r, 2, 5)):
            sums[r][near][1].wait_recv()
            sums[r][passed][1].wait_recv()
            cols = pl.ds(chunk * 512, 512)
            total = part[x, :, cols].astype(F32) + recv[6 * r + near].astype(F32)
            total = total + recv[6 * r + passed].astype(F32)
            out[:, cols] = (own[:, cols].astype(F32) + total).astype(BF16)

    for s in range(2):
        for copy in y_copies(s):
            copy.wait_send()
    z_copy.wait_send()
    for copy in w_partner + w_z + w_relay:
        copy.wait_send()
    for q in range(4):
        for copy in gated_other(q) + gated_mine(q):
            copy.wait_send()
    for r in range(4):
        for _, copy in sums[r]:
            copy.wait_send()


def shards(
    tokens,
    norm_gain,
    w_in,
    short_taps,
    filter_taps,
    filter_decay,
    skip_gain,
    w_out,
    slot_span,
    span_reset,
):
    fwd, inv = transforms()
    hbm = pl.BlockSpec(memory_space=pl.ANY)
    vmem = pl.BlockSpec(memory_space=pltpu.VMEM)
    smem = pl.BlockSpec(memory_space=pltpu.SMEM)
    return pl.pallas_call(
        kernel,
        out_shape=jax.ShapeDtypeStruct((128, 4096), BF16),
        in_specs=[hbm, vmem, hbm, vmem, vmem, vmem, vmem, hbm, vmem, vmem, smem, smem],
        out_specs=vmem,
        scratch_shapes=[
            pltpu.VMEM((2, 288, 4096), BF16),
            pltpu.VMEM((288, 4096), BF16),
            pltpu.VMEM((3, 4096, 256), BF16),
            pltpu.VMEM((3, 2, 1032, 256), F32),
            pltpu.VMEM((3, 128, 256), F32),
            pltpu.VMEM((8, HALO, 256), BF16),
            pltpu.VMEM((2, 2, HALO, 256), BF16),
            pltpu.VMEM((2048, 256), BF16),
            pltpu.VMEM((512, 1024), BF16),
            pltpu.VMEM((1024, 4096), BF16),
            pltpu.VMEM((4, 128, 4096), BF16),
            pltpu.VMEM((24, 128, 512), BF16),
            pltpu.VMEM((128, 4096), BF16),
            pltpu.VMEM((384, 256), BF16),
            pltpu.VMEM((256, 256), F32),
            pltpu.VMEM((2, 256, 256), BF16),
            pltpu.SemaphoreType.DMA((4,)),
            pltpu.SemaphoreType.DMA((3,)),
            pltpu.SemaphoreType.DMA((2,)),
            pltpu.SemaphoreType.DMA((6,)),
            pltpu.SemaphoreType.DMA((6,)),
            pltpu.SemaphoreType.DMA((1,)),
            pltpu.SemaphoreType.DMA((1,)),
            pltpu.SemaphoreType.DMA((12,)),
            pltpu.SemaphoreType.DMA((12,)),
            pltpu.SemaphoreType.DMA((24,)),
            pltpu.SemaphoreType.DMA((24,)),
            pltpu.SemaphoreType.DMA((24,)),
            pltpu.SemaphoreType.DMA((24,)),
        ],
        compiler_params=pltpu.CompilerParams(
            collective_id=0, has_side_effects=True, vmem_limit_bytes=60 * 1024 * 1024
        ),
    )(
        tokens,
        norm_gain.reshape(1, -1),
        jnp.transpose(w_in, (1, 0, 2)),
        short_taps,
        filter_taps,
        filter_decay.reshape(1, -1),
        skip_gain.reshape(1, -1),
        w_out,
        jnp.asarray(fwd),
        jnp.asarray(inv),
        slot_span,
        span_reset,
    )


def solution(mesh):
    in_specs = (
        P("ctx", None),
        P(),
        P(None, None, "tensor"),
        P(None, None, "tensor"),
        P(None, "tensor"),
        P("tensor"),
        P("tensor"),
        P("tensor", None),
        P(),
        P(),
    )
    out_specs = P(("ctx", "tensor"), None)
    return jax.shard_map(shards, mesh=mesh, in_specs=in_specs, out_specs=out_specs, check_vma=False)
```

```python
import jax
import jax.numpy as jnp
import numpy as np
from jax import lax
from jax.experimental import pallas as pl
from jax.experimental.pallas import tpu as pltpu
from jax.sharding import PartitionSpec as P

epsilon = 1e-06
F32 = jnp.float32
BF16 = jnp.bfloat16
MESH = pl.DeviceIdType.MESH
HALO = 144


def split(value):
    high = value.astype(BF16)
    low = (value - high.astype(F32)).astype(BF16)
    return high, low


def transforms():
    points = 256
    k = np.arange(128)[:, None]
    n = np.arange(points)[None, :]
    forward = np.zeros((points, points))
    forward[:128] = np.cos(2 * np.pi * k * n / points)
    forward[128:] = np.sin(2 * np.pi * k * n / points)
    forward[128] = np.cos(np.pi * n[0])
    weight = np.full((points, 1), 2.0 / points)
    weight[0] = weight[128] = 1.0 / points
    inverse = (forward * weight)[:, 128:].T

    def halves(matrix):
        high = matrix.astype(jnp.bfloat16)
        low = (matrix - high.astype(np.float64)).astype(jnp.bfloat16)
        return np.stack([high, low])

    return halves(forward), halves(inverse)


def dot(a, b):
    return jnp.dot(a, b, preferred_element_type=F32)


def kernel(
    tokens,
    gain,
    w_in,
    short,
    taps,
    decay,
    skip,
    w_out,
    fwd,
    inv,
    slot_span,
    span_reset,
    out,
    tok,
    scaled,
    win,
    pr,
    spec,
    column,
    across,
    gsend,
    grecv,
    wg,
    part,
    recv,
    own,
    mix,
    gate,
    prods,
    tok_sem,
    win_sem,
    loc_sem,
    y_send,
    y_recv,
    z_send,
    z_recv,
    g_send,
    g_recv,
    w_send,
    w_recv,
    r_send,
    r_recv,
):
    ctx = lax.axis_index("ctx")
    ten = lax.axis_index("tensor")
    y = ctx // 2
    zh = ctx % 2
    z = ten // 8
    x = (ten // 2) % 4
    core = ten % 2
    oz = 1 - z
    oc = 1 - core
    octx = y * 2 + 1 - zh
    right = (x + 1) % 4
    left = (x + 3) % 4
    far = (x + 2) % 4

    def place(z_, x_, c_):
        return z_ * 8 + x_ * 2 + c_

    partner = (ctx, place(z, x, oc))
    zsame = (ctx, place(oz, x, core))
    zcross = (ctx, place(oz, x, oc))
    zother = (octx, place(oz, x, core))
    zfar = (octx, ten)
    to_right = (ctx, place(z, right, core))
    to_left = (ctx, place(z, left, core))
    y_peers = [(((y + d) % 4) * 2 + zh, ten) for d in (2, 1, 3)]
    peers = [partner, zsame, zcross, zother, zfar, to_right, to_left] + y_peers

    first = [(oz, 880, 144), (z, 880, 144)]
    second = [(oz, 768, 112), (z, 768, 112)]

    def block_of(i):
        j = i - 2
        return jnp.where(j < 3, oz, z), 2 - j % 3

    def pieces_of(i):
        if isinstance(i, int) and i < 2:
            return (first, second)[i]
        s, q = block_of(i)
        return [(s, q * 256, 256)]

    def fetch(i):
        offset = 0
        copies = []
        for s, start, count in pieces_of(i):
            row = pl.multiple_of(s * 1024 + start, 16)
            index = (i % 2) * 2 + len(copies)
            copies.append(
                pltpu.make_async_copy(
                    tokens.at[pl.ds(row, count)],
                    tok.at[i % 2, pl.ds(offset, count)],
                    tok_sem.at[index],
                )
            )
            offset += count
        return copies

    def start(copies):
        for copy in copies:
            copy.start()

    def wait(copies):
        for copy in copies:
            copy.wait()

    barrier = pltpu.get_barrier_semaphore()
    for peer in peers:
        pl.semaphore_signal(barrier, inc=1, device_id=peer, device_id_type=MESH)
    own_group = z * 2 + core
    own_rows = pl.multiple_of(own_group * 256, 256)
    wg_copy = pltpu.make_async_copy(w_out, wg.at[pl.ds(own_rows, 256)], loc_sem.at[0])
    wg_copy.start()
    start(fetch(0))
    win_copies = [pltpu.make_async_copy(w_in.at[p], win.at[p], win_sem.at[p]) for p in range(3)]
    start(win_copies)
    start(fetch(1))
    tok_row = pl.multiple_of(ten * 128, 128)
    own_copy = pltpu.make_async_copy(tokens.at[pl.ds(tok_row, 128)], own, loc_sem.at[1])
    own_copy.start()
    wg_copy.wait()
    pl.semaphore_wait(barrier, len(peers))

    def w_copy(index, rows, chunk, peer):
        cols = pl.ds(chunk * 512, 512)
        return pltpu.make_async_remote_copy(
            src_ref=wg.at[pl.ds(rows, 256), cols],
            dst_ref=wg.at[pl.ds(rows, 256), cols],
            send_sem=w_send.at[index],
            recv_sem=w_recv.at[index],
            device_id=peer,
            device_id_type=MESH,
        )

    z_rows = pl.multiple_of((oz * 2 + core) * 256, 256)
    direct = (0, 1, 7)
    w_partner = [w_copy(c, own_rows, c, partner) for c in range(8)]
    w_z = [w_copy(8 + c, own_rows, c, zsame if c in direct else zother) for c in range(8)]
    w_relay = [w_copy(16 + c, z_rows, c, partner) for c in range(8)]

    def relay(chunks):
        for c in chunks:
            w_z[c].wait_recv()
            w_relay[c].start()

    start([w_z[0], w_z[4], w_z[1], w_z[5], w_z[2]])
    start([w_partner[c] for c in (0, 4, 1, 5, 2, 6, 3, 7)])

    lag = lax.broadcasted_iota(jnp.int32, (128, 256), 0)
    response = taps[...] * jnp.exp(-decay[...] * lag.astype(F32))
    response = response + jnp.where(lag == 0, skip[...], 0.0)
    r_high, r_low = split(response)
    spectrum = (
        dot(fwd[0, :, :128], r_high) + dot(fwd[1, :, :128], r_high) + dot(fwd[0, :, :128], r_low)
    )
    cos_part = spectrum[:128]
    sin_part = spectrum[128:]
    spec[0] = cos_part
    spec[1] = jnp.where(lag == 0, 0.0, sin_part)
    spec[2] = jnp.where(lag == 0, sin_part, cos_part)

    def prepare(i):
        slot = i % 2
        rows = sum(count for _, _, count in pieces_of(i))
        square = jnp.zeros((rows, 128), F32)
        for chunk in range(8):
            cols = pl.ds(chunk * 512, 512)
            value = tok[slot, pl.ds(0, rows), cols].astype(F32)
            scaled[pl.ds(0, rows), cols] = (value * gain[:, cols]).astype(BF16)
            value = value * value
            for lane in range(4):
                square = square + value[:, lane * 128 : lane * 128 + 128]
        return lax.rsqrt(jnp.sum(square, axis=1, keepdims=True) * (1.0 / 4096) + epsilon)

    def project_part(i, p, scale):
        layout = pieces_of(i)
        rows = sum(count for _, _, count in layout)
        value = dot(scaled[pl.ds(0, rows), :], win[p]) * scale
        offset = 0
        for s, begin, count in layout:
            row = pl.multiple_of(8 + begin, 8)
            pr[p, s, pl.ds(row, count), :] = value[offset : offset + count]
            offset += count

    def project(i):
        scale = prepare(i)
        for p in range(3):
            project_part(i, p, scale)

    def smooth(p, value, rows):
        return (
            short[0, pl.ds(p, 1), :] * value[8 : 8 + rows]
            + short[1, pl.ds(p, 1), :] * value[7 : 7 + rows]
            + short[2, pl.ds(p, 1), :] * value[6 : 6 + rows]
        )

    def y_copies(s):
        index = y * 2 + s
        return [
            pltpu.make_async_remote_copy(
                src_ref=column.at[index],
                dst_ref=column.at[index],
                send_sem=y_send.at[d * 2 + s],
                recv_sem=y_recv.at[d * 2 + s],
                device_id=y_peers[d],
                device_id_type=MESH,
            )
            for d in range(3)
        ]

    line = lax.broadcasted_iota(jnp.int32, (8, 256), 0)

    def send_tail(s):
        index = y * 2 + s
        key = smooth(1, pr[1, s, pl.ds(896, 136), :], 128)
        val = smooth(2, pr[2, s, pl.ds(896, 136), :], 128)
        column[index, pl.ds(0, 128), :] = (key * val).astype(BF16)
        last = [pr[p, s, pl.ds(1024, 8), :] for p in range(3)]
        pair = jnp.where(line >= 6, last[0], pltpu.roll(last[1], 6, 0))
        column[index, pl.ds(128, 16), :] = jnp.concatenate([pair, last[2]], axis=0).astype(BF16)
        start(y_copies(s))

    def wanted(holder, s):
        span = slot_span[2 * holder + s]
        index = jnp.int32(0)
        half = jnp.int32(0)
        for j in range(16):
            hit = slot_span[j] == span - 1
            index = index + jnp.where(hit, (j // 4) * 2 + j % 2, 0)
            half = half + jnp.where(hit, (j // 2) % 2, 0)
        used = jnp.logical_and(span > 0, span_reset[span] == 0)
        return index, half, used

    z_copy = pltpu.make_async_remote_copy(
        src_ref=across.at[0],
        dst_ref=across.at[1],
        send_sem=z_send.at[0],
        recv_sem=z_recv.at[0],
        device_id=zfar,
        device_id_type=MESH,
    )

    def send_across():
        for s in range(2):
            for copy in y_copies(s):
                copy.wait_recv()
        for s in range(2):
            index, _, _ = wanted(octx, s)
            across[0, s] = column[index]
        z_copy.start()

    def to_spectrum(window):
        freq = dot(fwd[0], window)
        a = freq[:128]
        b = freq[128:]
        prod = jnp.concatenate([a * spec[0] - b * spec[1], a * spec[1] + b * spec[2]], axis=0)
        return prod.astype(BF16)

    def convolve(mixed, query):
        mixed = mixed.astype(BF16)
        outs = [dot(inv[0], to_spectrum(mixed[w * 128 : w * 128 + 256])) for w in range(2)]
        return (query * jnp.concatenate(outs, axis=0)).astype(BF16)

    own_cols = pl.ds(pl.multiple_of(own_group * 256, 256), 256)

    def gated_copy(index, send_row, peer, q):
        return pltpu.make_async_remote_copy(
            src_ref=gsend.at[pl.ds(send_row, 128)],
            dst_ref=grecv.at[pl.ds(pl.multiple_of(q * 128, 128), 128), own_cols],
            send_sem=g_send.at[index * 4 + q],
            recv_sem=g_recv.at[index * 4 + q],
            device_id=peer,
            device_id_type=MESH,
        )

    def gated_other(q):
        base = pl.multiple_of(q * 256, 256)
        same_row = pl.multiple_of(base + core * 128, 128)
        cross_row = pl.multiple_of(base + oc * 128, 128)
        return [gated_copy(0, same_row, zsame, q), gated_copy(1, cross_row, zcross, q)]

    def gated_mine(q):
        row = pl.multiple_of(1024 + q * 256 + oc * 128, 128)
        return [gated_copy(2, row, partner, q)]

    def keep(q):
        row = pl.multiple_of(1024 + q * 256 + core * 128, 128)
        grecv[pl.ds(pl.multiple_of(q * 128, 128), 128), own_cols] = gsend[pl.ds(row, 128), :]

    def smooth_block(role, q):
        s = jnp.where(role == 0, oz, z)
        wide = pl.ds(pl.multiple_of(q * 256 - 128, 128), 392)
        narrow = pl.ds(pl.multiple_of(q * 256, 256), 264)
        key = smooth(1, pr[1, s, wide, :], 384)
        val = smooth(2, pr[2, s, wide, :], 384)
        return key * val, smooth(0, pr[0, s, narrow, :], 256)

    def filter_block(role, q):
        row = pl.multiple_of(role * 1024 + q * 256, 256)
        gsend[pl.ds(row, 256), :] = convolve(*smooth_block(role, q))

    def filter_and_project(role, q, i):
        row = role * 1024 + q * 256
        mixed, query = smooth_block(role, q)
        mix[...] = mixed.astype(BF16)
        gate[...] = query
        scale = prepare(i)
        project_part(i, 0, scale)
        for w in range(2):
            prods[w] = to_spectrum(mix[pl.ds(w * 128, 256), :])
        project_part(i, 1, scale)
        for w in range(2):
            half = pl.ds(pl.multiple_of(row + w * 128, 128), 128)
            gsend[half, :] = (gate[pl.ds(w * 128, 128), :] * dot(inv[0], prods[w])).astype(BF16)
        project_part(i, 2, scale)

    def filter_first(role):
        s = oz if role == 0 else z
        index, half, used = wanted(ctx, s)
        mask_here = jnp.where(jnp.logical_and(used, half == zh), 1.0, 0.0)
        mask_across = jnp.where(jnp.logical_and(used, half != zh), 1.0, 0.0)
        before = column[index].astype(F32) * mask_here + across[1, s].astype(F32) * mask_across
        pair = before[128:136]
        pr[0, s, pl.ds(0, 8), :] = pair
        pr[1, s, pl.ds(0, 8), :] = pltpu.roll(pair, 2, 0)
        pr[2, s, pl.ds(0, 8), :] = before[136:144]
        window = pl.ds(0, 264)
        key = smooth(1, pr[1, s, window, :], 256)
        val = smooth(2, pr[2, s, window, :], 256)
        query = smooth(0, pr[0, s, window, :], 256)
        mixed = jnp.concatenate([before[:128], key * val], axis=0)
        gsend[pl.ds(role * 1024, 256), :] = convolve(mixed, query)

    wait(fetch(0))
    scale = prepare(0)
    start(fetch(2))
    for p in range(3):
        win_copies[p].wait()
        project_part(0, p, scale)
    for s in range(2):
        send_tail(s)
    wait(fetch(1))
    project(1)
    start(fetch(3))
    wait(fetch(2))
    project(2)

    def main_step(i, carry):
        j = i - 3
        role = jnp.where(j < 3, 0, 1)
        q = 3 - j % 3

        @pl.when(i < 7)
        def _():
            start(fetch(i + 1))

        wait(fetch(i))
        filter_and_project(role, q, i)

        @pl.when(j < 3)
        def _():
            start(gated_other(q))

        @pl.when(j >= 3)
        def _():
            keep(q)
            start(gated_mine(q))

        @pl.when(j == 0)
        def _():
            relay((0, 4))

        @pl.when(j == 1)
        def _():
            relay((1, 5))
            w_z[6].start()

        @pl.when(j == 2)
        def _():
            send_across()
            start([w_z[3], w_z[7]])

        @pl.when(j == 3)
        def _():
            relay((2,))

        return carry

    lax.fori_loop(3, 8, main_step, 0)
    filter_block(1, jnp.int32(1))
    keep(1)
    start(gated_mine(1))

    def r_copy(index, block, chunk, peer):
        cols = pl.ds(chunk * 512, 512)
        return pltpu.make_async_remote_copy(
            src_ref=part.at[block, :, cols],
            dst_ref=recv.at[index],
            send_sem=r_send.at[index],
            recv_sem=r_recv.at[index],
            device_id=peer,
            device_id_type=MESH,
        )

    sums = []
    for r in range(4):
        a, b = r, 4 + r
        sums.append(
            [
                (far, r_copy(6 * r + 0, far, a, to_right)),
                (far, r_copy(6 * r + 1, far, b, to_left)),
                (right, r_copy(6 * r + 2, right, b, to_right)),
                (left, r_copy(6 * r + 3, left, a, to_left)),
                (right, r_copy(6 * r + 4, right, a, to_right)),
                (left, r_copy(6 * r + 5, left, b, to_left)),
            ]
        )

    def multiply(r, begin, blocks):
        def columns(k, carry):
            cols = pl.ds(pl.multiple_of((k // 2) * 2048 + r * 512 + (k % 2) * 256, 256), 256)
            value = dot(grecv[pl.ds(begin * 128, blocks * 128), :], wg[:, cols]).astype(BF16)
            for q in range(blocks):
                part[begin + q, :, cols] = value[q * 128 : q * 128 + 128]
            return carry

        lax.fori_loop(0, 4, columns, 0)

    def send_own(r, ready):
        for block, copy in sums[r][:4]:
            if ready is None:
                copy.start()
            else:

                @pl.when(ready(block))
                def _(copy=copy):
                    copy.start()

    def add_and_send(r, index):
        block, copy = sums[r][4 + index]
        sums[r][index][1].wait_recv()
        cols = pl.ds((r + 4 * index) * 512, 512)
        part[block, :, cols] = (
            part[block, :, cols].astype(F32) + recv[6 * r + index].astype(F32)
        ).astype(BF16)
        copy.start()

    def pass_on(r, ready):
        for index in range(2):
            if ready is None:
                add_and_send(r, index)
            else:

                @pl.when(ready(sums[r][4 + index][0]))
                def _(index=index):
                    add_and_send(r, index)

    def w_ready(r):
        for c in (r, 4 + r):
            w_partner[c].wait_recv()
            w_relay[c].wait_recv()

    early = lambda block: block != 0
    late = lambda block: block == 0

    def gated_ready(q):
        for copy in gated_other(q) + gated_mine(q):
            copy.wait_recv()

    for q in (3, 2, 1):
        gated_ready(q)
    for r in range(2):
        w_ready(r)
        multiply(r, 1, 3)
        send_own(r, early)

    z_copy.wait_recv()
    filter_first(0)
    start(gated_other(0))
    filter_first(1)
    keep(0)
    start(gated_mine(0))
    relay((6,))
    w_ready(2)
    multiply(2, 1, 3)
    send_own(2, early)
    gated_ready(0)
    for r in range(3):
        multiply(r, 0, 1)
        send_own(r, late)
    relay((3, 7))
    for r in range(2):
        pass_on(r, early)
    w_ready(3)
    multiply(3, 0, 4)
    send_own(3, None)
    for r in range(2):
        pass_on(r, late)
    for r in (2, 3):
        pass_on(r, None)
    own_copy.wait()
    for r in range(4):
        for chunk, near, passed in ((r, 3, 4), (4 + r, 2, 5)):
            sums[r][near][1].wait_recv()
            sums[r][passed][1].wait_recv()
            cols = pl.ds(chunk * 512, 512)
            total = part[x, :, cols].astype(F32) + recv[6 * r + near].astype(F32)
            total = total + recv[6 * r + passed].astype(F32)
            out[:, cols] = (own[:, cols].astype(F32) + total).astype(BF16)

    for s in range(2):
        for copy in y_copies(s):
            copy.wait_send()
    z_copy.wait_send()
    for copy in w_partner + w_z + w_relay:
        copy.wait_send()
    for q in range(4):
        for copy in gated_other(q) + gated_mine(q):
            copy.wait_send()
    for r in range(4):
        for _, copy in sums[r]:
            copy.wait_send()


def shards(
    tokens,
    norm_gain,
    w_in,
    short_taps,
    filter_taps,
    filter_decay,
    skip_gain,
    w_out,
    slot_span,
    span_reset,
):
    fwd, inv = transforms()
    hbm = pl.BlockSpec(memory_space=pl.ANY)
    vmem = pl.BlockSpec(memory_space=pltpu.VMEM)
    smem = pl.BlockSpec(memory_space=pltpu.SMEM)
    return pl.pallas_call(
        kernel,
        out_shape=jax.ShapeDtypeStruct((128, 4096), BF16),
        in_specs=[hbm, vmem, hbm, vmem, vmem, vmem, vmem, hbm, vmem, vmem, smem, smem],
        out_specs=vmem,
        scratch_shapes=[
            pltpu.VMEM((2, 288, 4096), BF16),
            pltpu.VMEM((288, 4096), BF16),
            pltpu.VMEM((3, 4096, 256), BF16),
            pltpu.VMEM((3, 2, 1032, 256), F32),
            pltpu.VMEM((3, 128, 256), F32),
            pltpu.VMEM((8, HALO, 256), BF16),
            pltpu.VMEM((2, 2, HALO, 256), BF16),
            pltpu.VMEM((2048, 256), BF16),
            pltpu.VMEM((512, 1024), BF16),
            pltpu.VMEM((1024, 4096), BF16),
            pltpu.VMEM((4, 128, 4096), BF16),
            pltpu.VMEM((24, 128, 512), BF16),
            pltpu.VMEM((128, 4096), BF16),
            pltpu.VMEM((384, 256), BF16),
            pltpu.VMEM((256, 256), F32),
            pltpu.VMEM((2, 256, 256), BF16),
            pltpu.SemaphoreType.DMA((4,)),
            pltpu.SemaphoreType.DMA((3,)),
            pltpu.SemaphoreType.DMA((2,)),
            pltpu.SemaphoreType.DMA((6,)),
            pltpu.SemaphoreType.DMA((6,)),
            pltpu.SemaphoreType.DMA((1,)),
            pltpu.SemaphoreType.DMA((1,)),
            pltpu.SemaphoreType.DMA((12,)),
            pltpu.SemaphoreType.DMA((12,)),
            pltpu.SemaphoreType.DMA((24,)),
            pltpu.SemaphoreType.DMA((24,)),
            pltpu.SemaphoreType.DMA((24,)),
            pltpu.SemaphoreType.DMA((24,)),
        ],
        compiler_params=pltpu.CompilerParams(
            collective_id=0, has_side_effects=True, vmem_limit_bytes=60 * 1024 * 1024
        ),
    )(
        tokens,
        norm_gain.reshape(1, -1),
        jnp.transpose(w_in, (1, 0, 2)),
        short_taps,
        filter_taps,
        filter_decay.reshape(1, -1),
        skip_gain.reshape(1, -1),
        w_out,
        jnp.asarray(fwd),
        jnp.asarray(inv),
        slot_span,
        span_reset,
    )


def solution(mesh):
    in_specs = (
        P("ctx", None),
        P(),
        P(None, None, "tensor"),
        P(None, None, "tensor"),
        P(None, "tensor"),
        P("tensor"),
        P("tensor"),
        P("tensor", None),
        P(),
        P(),
    )
    out_specs = P(("ctx", "tensor"), None)
    return jax.shard_map(shards, mesh=mesh, in_specs=in_specs, out_specs=out_specs, check_vma=False)
```

```python
import jax
import jax.numpy as jnp
import numpy as np
from jax import lax
from jax.experimental import pallas as pl
from jax.experimental.pallas import tpu as pltpu
from jax.sharding import PartitionSpec as P

epsilon = 1e-06
F32 = jnp.float32
BF16 = jnp.bfloat16
MESH = pl.DeviceIdType.MESH
HALO = 144


def split(value):
    high = value.astype(BF16)
    low = (value - high.astype(F32)).astype(BF16)
    return high, low


def transforms():
    points = 256
    k = np.arange(128)[:, None]
    n = np.arange(points)[None, :]
    forward = np.zeros((points, points))
    forward[:128] = np.cos(2 * np.pi * k * n / points)
    forward[128:] = np.sin(2 * np.pi * k * n / points)
    forward[128] = np.cos(np.pi * n[0])
    weight = np.full((points, 1), 2.0 / points)
    weight[0] = weight[128] = 1.0 / points
    inverse = (forward * weight)[:, 128:].T

    def halves(matrix):
        high = matrix.astype(jnp.bfloat16)
        low = (matrix - high.astype(np.float64)).astype(jnp.bfloat16)
        return np.stack([high, low])

    return halves(forward), halves(inverse)


def dot(a, b):
    return jnp.dot(a, b, preferred_element_type=F32)


def kernel(
    tokens,
    gain,
    w_in,
    short,
    taps,
    decay,
    skip,
    w_out,
    fwd,
    inv,
    slot_span,
    span_reset,
    out,
    tok,
    scaled,
    win,
    pr,
    spec,
    column,
    across,
    gsend,
    grecv,
    wg,
    part,
    recv,
    own,
    mix,
    gate,
    prods,
    tok_sem,
    win_sem,
    loc_sem,
    y_send,
    y_recv,
    z_send,
    z_recv,
    g_send,
    g_recv,
    w_send,
    w_recv,
    r_send,
    r_recv,
):
    ctx = lax.axis_index("ctx")
    ten = lax.axis_index("tensor")
    y = ctx // 2
    zh = ctx % 2
    z = ten // 8
    x = (ten // 2) % 4
    core = ten % 2
    oz = 1 - z
    oc = 1 - core
    octx = y * 2 + 1 - zh
    right = (x + 1) % 4
    left = (x + 3) % 4
    far = (x + 2) % 4

    def place(z_, x_, c_):
        return z_ * 8 + x_ * 2 + c_

    partner = (ctx, place(z, x, oc))
    zsame = (ctx, place(oz, x, core))
    zcross = (ctx, place(oz, x, oc))
    zother = (octx, place(oz, x, core))
    zfar = (octx, ten)
    to_right = (ctx, place(z, right, core))
    to_left = (ctx, place(z, left, core))
    y_peers = [(((y + d) % 4) * 2 + zh, ten) for d in (2, 1, 3)]
    peers = [partner, zsame, zcross, zother, zfar, to_right, to_left] + y_peers

    first = [(oz, 880, 144), (z, 880, 144)]
    second = [(oz, 768, 112), (z, 768, 112)]

    def block_of(i):
        j = i - 2
        return jnp.where(j < 3, oz, z), 2 - j % 3

    def pieces_of(i):
        if isinstance(i, int) and i < 2:
            return (first, second)[i]
        s, q = block_of(i)
        return [(s, q * 256, 256)]

    def fetch(i):
        offset = 0
        copies = []
        for s, start, count in pieces_of(i):
            row = pl.multiple_of(s * 1024 + start, 16)
            index = (i % 2) * 2 + len(copies)
            copies.append(
                pltpu.make_async_copy(
                    tokens.at[pl.ds(row, count)],
                    tok.at[i % 2, pl.ds(offset, count)],
                    tok_sem.at[index],
                )
            )
            offset += count
        return copies

    def start(copies):
        for copy in copies:
            copy.start()

    def wait(copies):
        for copy in copies:
            copy.wait()

    barrier = pltpu.get_barrier_semaphore()
    for peer in peers:
        pl.semaphore_signal(barrier, inc=1, device_id=peer, device_id_type=MESH)
    own_group = z * 2 + core
    own_rows = pl.multiple_of(own_group * 256, 256)
    wg_copy = pltpu.make_async_copy(w_out, wg.at[pl.ds(own_rows, 256)], loc_sem.at[0])
    wg_copy.start()
    start(fetch(0))
    win_copies = [pltpu.make_async_copy(w_in.at[p], win.at[p], win_sem.at[p]) for p in range(3)]
    start(win_copies)
    start(fetch(1))
    tok_row = pl.multiple_of(ten * 128, 128)
    own_copy = pltpu.make_async_copy(tokens.at[pl.ds(tok_row, 128)], own, loc_sem.at[1])
    own_copy.start()
    wg_copy.wait()
    pl.semaphore_wait(barrier, len(peers))

    def w_copy(index, rows, chunk, peer):
        cols = pl.ds(chunk * 512, 512)
        return pltpu.make_async_remote_copy(
            src_ref=wg.at[pl.ds(rows, 256), cols],
            dst_ref=wg.at[pl.ds(rows, 256), cols],
            send_sem=w_send.at[index],
            recv_sem=w_recv.at[index],
            device_id=peer,
            device_id_type=MESH,
        )

    z_rows = pl.multiple_of((oz * 2 + core) * 256, 256)
    direct = (0, 1, 7)
    w_partner = [w_copy(c, own_rows, c, partner) for c in range(8)]
    w_z = [w_copy(8 + c, own_rows, c, zsame if c in direct else zother) for c in range(8)]
    w_relay = [w_copy(16 + c, z_rows, c, partner) for c in range(8)]

    def relay(chunks):
        for c in chunks:
            w_z[c].wait_recv()
            w_relay[c].start()

    start([w_z[0], w_z[4], w_z[1], w_z[5], w_z[2]])
    start([w_partner[c] for c in (0, 4, 1, 5, 2, 6, 3, 7)])

    lag = lax.broadcasted_iota(jnp.int32, (128, 256), 0)
    response = taps[...] * jnp.exp(-decay[...] * lag.astype(F32))
    response = response + jnp.where(lag == 0, skip[...], 0.0)
    r_high, r_low = split(response)
    spectrum = (
        dot(fwd[0, :, :128], r_high) + dot(fwd[1, :, :128], r_high) + dot(fwd[0, :, :128], r_low)
    )
    cos_part = spectrum[:128]
    sin_part = spectrum[128:]
    spec[0] = cos_part
    spec[1] = jnp.where(lag == 0, 0.0, sin_part)
    spec[2] = jnp.where(lag == 0, sin_part, cos_part)

    def prepare(i):
        slot = i % 2
        rows = sum(count for _, _, count in pieces_of(i))
        square = jnp.zeros((rows, 128), F32)
        for chunk in range(8):
            cols = pl.ds(chunk * 512, 512)
            value = tok[slot, pl.ds(0, rows), cols].astype(F32)
            scaled[pl.ds(0, rows), cols] = (value * gain[:, cols]).astype(BF16)
            value = value * value
            for lane in range(4):
                square = square + value[:, lane * 128 : lane * 128 + 128]
        return lax.rsqrt(jnp.sum(square, axis=1, keepdims=True) * (1.0 / 4096) + epsilon)

    def project_part(i, p, scale):
        layout = pieces_of(i)
        rows = sum(count for _, _, count in layout)
        value = dot(scaled[pl.ds(0, rows), :], win[p]) * scale
        offset = 0
        for s, begin, count in layout:
            row = pl.multiple_of(8 + begin, 8)
            pr[p, s, pl.ds(row, count), :] = value[offset : offset + count]
            offset += count

    def project(i):
        scale = prepare(i)
        for p in range(3):
            project_part(i, p, scale)

    def smooth(p, value, rows):
        return (
            short[0, pl.ds(p, 1), :] * value[8 : 8 + rows]
            + short[1, pl.ds(p, 1), :] * value[7 : 7 + rows]
            + short[2, pl.ds(p, 1), :] * value[6 : 6 + rows]
        )

    def y_copies(s):
        index = y * 2 + s
        return [
            pltpu.make_async_remote_copy(
                src_ref=column.at[index],
                dst_ref=column.at[index],
                send_sem=y_send.at[d * 2 + s],
                recv_sem=y_recv.at[d * 2 + s],
                device_id=y_peers[d],
                device_id_type=MESH,
            )
            for d in range(3)
        ]

    line = lax.broadcasted_iota(jnp.int32, (8, 256), 0)

    def send_tail(s):
        index = y * 2 + s
        key = smooth(1, pr[1, s, pl.ds(896, 136), :], 128)
        val = smooth(2, pr[2, s, pl.ds(896, 136), :], 128)
        column[index, pl.ds(0, 128), :] = (key * val).astype(BF16)
        last = [pr[p, s, pl.ds(1024, 8), :] for p in range(3)]
        pair = jnp.where(line >= 6, last[0], pltpu.roll(last[1], 6, 0))
        column[index, pl.ds(128, 16), :] = jnp.concatenate([pair, last[2]], axis=0).astype(BF16)
        start(y_copies(s))

    def wanted(holder, s):
        span = slot_span[2 * holder + s]
        index = jnp.int32(0)
        half = jnp.int32(0)
        for j in range(16):
            hit = slot_span[j] == span - 1
            index = index + jnp.where(hit, (j // 4) * 2 + j % 2, 0)
            half = half + jnp.where(hit, (j // 2) % 2, 0)
        used = jnp.logical_and(span > 0, span_reset[span] == 0)
        return index, half, used

    z_copy = pltpu.make_async_remote_copy(
        src_ref=across.at[0],
        dst_ref=across.at[1],
        send_sem=z_send.at[0],
        recv_sem=z_recv.at[0],
        device_id=zfar,
        device_id_type=MESH,
    )

    def send_across():
        for s in range(2):
            for copy in y_copies(s):
                copy.wait_recv()
        for s in range(2):
            index, _, _ = wanted(octx, s)
            across[0, s] = column[index]
        z_copy.start()

    def to_spectrum(window):
        freq = dot(fwd[0], window)
        a = freq[:128]
        b = freq[128:]
        prod = jnp.concatenate([a * spec[0] - b * spec[1], a * spec[1] + b * spec[2]], axis=0)
        return prod.astype(BF16)

    def convolve(mixed, query):
        mixed = mixed.astype(BF16)
        outs = [dot(inv[0], to_spectrum(mixed[w * 128 : w * 128 + 256])) for w in range(2)]
        return (query * jnp.concatenate(outs, axis=0)).astype(BF16)

    own_cols = pl.ds(pl.multiple_of(own_group * 256, 256), 256)

    def gated_copy(index, send_row, peer, q):
        return pltpu.make_async_remote_copy(
            src_ref=gsend.at[pl.ds(send_row, 128)],
            dst_ref=grecv.at[pl.ds(pl.multiple_of(q * 128, 128), 128), own_cols],
            send_sem=g_send.at[index * 4 + q],
            recv_sem=g_recv.at[index * 4 + q],
            device_id=peer,
            device_id_type=MESH,
        )

    def gated_other(q):
        base = pl.multiple_of(q * 256, 256)
        same_row = pl.multiple_of(base + core * 128, 128)
        cross_row = pl.multiple_of(base + oc * 128, 128)
        return [gated_copy(0, same_row, zsame, q), gated_copy(1, cross_row, zcross, q)]

    def gated_mine(q):
        row = pl.multiple_of(1024 + q * 256 + oc * 128, 128)
        return [gated_copy(2, row, partner, q)]

    def keep(q):
        row = pl.multiple_of(1024 + q * 256 + core * 128, 128)
        grecv[pl.ds(pl.multiple_of(q * 128, 128), 128), own_cols] = gsend[pl.ds(row, 128), :]

    def smooth_block(role, q):
        s = jnp.where(role == 0, oz, z)
        wide = pl.ds(pl.multiple_of(q * 256 - 128, 128), 392)
        narrow = pl.ds(pl.multiple_of(q * 256, 256), 264)
        key = smooth(1, pr[1, s, wide, :], 384)
        val = smooth(2, pr[2, s, wide, :], 384)
        return key * val, smooth(0, pr[0, s, narrow, :], 256)

    def filter_block(role, q):
        row = pl.multiple_of(role * 1024 + q * 256, 256)
        gsend[pl.ds(row, 256), :] = convolve(*smooth_block(role, q))

    def filter_and_project(role, q, i):
        row = role * 1024 + q * 256
        mixed, query = smooth_block(role, q)
        mix[...] = mixed.astype(BF16)
        gate[...] = query
        scale = prepare(i)
        project_part(i, 0, scale)
        for w in range(2):
            prods[w] = to_spectrum(mix[pl.ds(w * 128, 256), :])
        project_part(i, 1, scale)
        for w in range(2):
            half = pl.ds(pl.multiple_of(row + w * 128, 128), 128)
            gsend[half, :] = (gate[pl.ds(w * 128, 128), :] * dot(inv[0], prods[w])).astype(BF16)
        project_part(i, 2, scale)

    def filter_first(role):
        s = oz if role == 0 else z
        index, half, used = wanted(ctx, s)
        mask_here = jnp.where(jnp.logical_and(used, half == zh), 1.0, 0.0)
        mask_across = jnp.where(jnp.logical_and(used, half != zh), 1.0, 0.0)
        before = column[index].astype(F32) * mask_here + across[1, s].astype(F32) * mask_across
        pair = before[128:136]
        pr[0, s, pl.ds(0, 8), :] = pair
        pr[1, s, pl.ds(0, 8), :] = pltpu.roll(pair, 2, 0)
        pr[2, s, pl.ds(0, 8), :] = before[136:144]
        window = pl.ds(0, 264)
        key = smooth(1, pr[1, s, window, :], 256)
        val = smooth(2, pr[2, s, window, :], 256)
        query = smooth(0, pr[0, s, window, :], 256)
        mixed = jnp.concatenate([before[:128], key * val], axis=0)
        gsend[pl.ds(role * 1024, 256), :] = convolve(mixed, query)

    wait(fetch(0))
    scale = prepare(0)
    start(fetch(2))
    for p in range(3):
        win_copies[p].wait()
        project_part(0, p, scale)
    for s in range(2):
        send_tail(s)
    wait(fetch(1))
    project(1)
    start(fetch(3))
    wait(fetch(2))
    project(2)

    def main_step(i, carry):
        j = i - 3
        role = jnp.where(j < 3, 0, 1)
        q = 3 - j % 3

        @pl.when(i < 7)
        def _():
            start(fetch(i + 1))

        wait(fetch(i))
        filter_and_project(role, q, i)

        @pl.when(j < 3)
        def _():
            start(gated_other(q))

        @pl.when(j >= 3)
        def _():
            keep(q)
            start(gated_mine(q))

        @pl.when(j == 0)
        def _():
            relay((0, 4))

        @pl.when(j == 1)
        def _():
            relay((1, 5))
            w_z[6].start()

        @pl.when(j == 2)
        def _():
            send_across()
            start([w_z[3], w_z[7]])

        @pl.when(j == 3)
        def _():
            relay((2,))

        return carry

    lax.fori_loop(3, 8, main_step, 0)
    filter_block(1, jnp.int32(1))
    keep(1)
    start(gated_mine(1))

    def r_copy(index, block, chunk, peer):
        cols = pl.ds(chunk * 512, 512)
        return pltpu.make_async_remote_copy(
            src_ref=part.at[block, :, cols],
            dst_ref=recv.at[index],
            send_sem=r_send.at[index],
            recv_sem=r_recv.at[index],
            device_id=peer,
            device_id_type=MESH,
        )

    sums = []
    for r in range(4):
        a, b = r, 4 + r
        sums.append(
            [
                (far, r_copy(6 * r + 0, far, a, to_right)),
                (far, r_copy(6 * r + 1, far, b, to_left)),
                (right, r_copy(6 * r + 2, right, b, to_right)),
                (left, r_copy(6 * r + 3, left, a, to_left)),
                (right, r_copy(6 * r + 4, right, a, to_right)),
                (left, r_copy(6 * r + 5, left, b, to_left)),
            ]
        )

    def multiply(r, begin, blocks):
        def columns(k, carry):
            cols = pl.ds(pl.multiple_of((k // 2) * 2048 + r * 512 + (k % 2) * 256, 256), 256)
            value = dot(grecv[pl.ds(begin * 128, blocks * 128), :], wg[:, cols]).astype(BF16)
            for q in range(blocks):
                part[begin + q, :, cols] = value[q * 128 : q * 128 + 128]
            return carry

        lax.fori_loop(0, 4, columns, 0)

    def send_own(r, ready):
        for block, copy in sums[r][:4]:
            if ready is None:
                copy.start()
            else:

                @pl.when(ready(block))
                def _(copy=copy):
                    copy.start()

    def add_and_send(r, index):
        block, copy = sums[r][4 + index]
        sums[r][index][1].wait_recv()
        cols = pl.ds((r + 4 * index) * 512, 512)
        part[block, :, cols] = (
            part[block, :, cols].astype(F32) + recv[6 * r + index].astype(F32)
        ).astype(BF16)
        copy.start()

    def pass_on(r, ready):
        for index in range(2):
            if ready is None:
                add_and_send(r, index)
            else:

                @pl.when(ready(sums[r][4 + index][0]))
                def _(index=index):
                    add_and_send(r, index)

    def w_ready(r):
        for c in (r, 4 + r):
            w_partner[c].wait_recv()
            w_relay[c].wait_recv()

    early = lambda block: block != 0
    late = lambda block: block == 0

    def gated_ready(q):
        for copy in gated_other(q) + gated_mine(q):
            copy.wait_recv()

    for q in (3, 2, 1):
        gated_ready(q)
    for r in range(2):
        w_ready(r)
        multiply(r, 1, 3)
        send_own(r, early)

    relay((6,))
    z_copy.wait_recv()
    filter_first(0)
    start(gated_other(0))
    filter_first(1)
    keep(0)
    start(gated_mine(0))
    w_ready(2)
    multiply(2, 1, 3)
    send_own(2, early)
    relay((7,))
    gated_ready(0)
    for r in range(3):
        multiply(r, 0, 1)
        send_own(r, late)
        if r == 1:
            relay((3,))
    for r in range(2):
        pass_on(r, early)
    w_ready(3)
    multiply(3, 0, 4)
    send_own(3, None)
    for r in range(2):
        pass_on(r, late)
    for r in (2, 3):
        pass_on(r, None)
    own_copy.wait()
    for r in range(4):
        for chunk, near, passed in ((r, 3, 4), (4 + r, 2, 5)):
            sums[r][near][1].wait_recv()
            sums[r][passed][1].wait_recv()
            cols = pl.ds(chunk * 512, 512)
            total = part[x, :, cols].astype(F32) + recv[6 * r + near].astype(F32)
            total = total + recv[6 * r + passed].astype(F32)
            out[:, cols] = (own[:, cols].astype(F32) + total).astype(BF16)

    for s in range(2):
        for copy in y_copies(s):
            copy.wait_send()
    z_copy.wait_send()
    for copy in w_partner + w_z + w_relay:
        copy.wait_send()
    for q in range(4):
        for copy in gated_other(q) + gated_mine(q):
            copy.wait_send()
    for r in range(4):
        for _, copy in sums[r]:
            copy.wait_send()


def shards(
    tokens,
    norm_gain,
    w_in,
    short_taps,
    filter_taps,
    filter_decay,
    skip_gain,
    w_out,
    slot_span,
    span_reset,
):
    fwd, inv = transforms()
    hbm = pl.BlockSpec(memory_space=pl.ANY)
    vmem = pl.BlockSpec(memory_space=pltpu.VMEM)
    smem = pl.BlockSpec(memory_space=pltpu.SMEM)
    return pl.pallas_call(
        kernel,
        out_shape=jax.ShapeDtypeStruct((128, 4096), BF16),
        in_specs=[hbm, vmem, hbm, vmem, vmem, vmem, vmem, hbm, vmem, vmem, smem, smem],
        out_specs=vmem,
        scratch_shapes=[
            pltpu.VMEM((2, 288, 4096), BF16),
            pltpu.VMEM((288, 4096), BF16),
            pltpu.VMEM((3, 4096, 256), BF16),
            pltpu.VMEM((3, 2, 1032, 256), F32),
            pltpu.VMEM((3, 128, 256), F32),
            pltpu.VMEM((8, HALO, 256), BF16),
            pltpu.VMEM((2, 2, HALO, 256), BF16),
            pltpu.VMEM((2048, 256), BF16),
            pltpu.VMEM((512, 1024), BF16),
            pltpu.VMEM((1024, 4096), BF16),
            pltpu.VMEM((4, 128, 4096), BF16),
            pltpu.VMEM((24, 128, 512), BF16),
            pltpu.VMEM((128, 4096), BF16),
            pltpu.VMEM((384, 256), BF16),
            pltpu.VMEM((256, 256), F32),
            pltpu.VMEM((2, 256, 256), BF16),
            pltpu.SemaphoreType.DMA((4,)),
            pltpu.SemaphoreType.DMA((3,)),
            pltpu.SemaphoreType.DMA((2,)),
            pltpu.SemaphoreType.DMA((6,)),
            pltpu.SemaphoreType.DMA((6,)),
            pltpu.SemaphoreType.DMA((1,)),
            pltpu.SemaphoreType.DMA((1,)),
            pltpu.SemaphoreType.DMA((12,)),
            pltpu.SemaphoreType.DMA((12,)),
            pltpu.SemaphoreType.DMA((24,)),
            pltpu.SemaphoreType.DMA((24,)),
            pltpu.SemaphoreType.DMA((24,)),
            pltpu.SemaphoreType.DMA((24,)),
        ],
        compiler_params=pltpu.CompilerParams(
            collective_id=0, has_side_effects=True, vmem_limit_bytes=60 * 1024 * 1024
        ),
    )(
        tokens,
        norm_gain.reshape(1, -1),
        jnp.transpose(w_in, (1, 0, 2)),
        short_taps,
        filter_taps,
        filter_decay.reshape(1, -1),
        skip_gain.reshape(1, -1),
        w_out,
        jnp.asarray(fwd),
        jnp.asarray(inv),
        slot_span,
        span_reset,
    )


def solution(mesh):
    in_specs = (
        P("ctx", None),
        P(),
        P(None, None, "tensor"),
        P(None, None, "tensor"),
        P(None, "tensor"),
        P("tensor"),
        P("tensor"),
        P("tensor", None),
        P(),
        P(),
    )
    out_specs = P(("ctx", "tensor"), None)
    return jax.shard_map(shards, mesh=mesh, in_specs=in_specs, out_specs=out_specs, check_vma=False)
```
